32 devices in a mesh: groups: 2 (over y), prefix: 4 (over z), heads: 2 (over x), sub: 2 (over core).
Axes of the slice: x: 2, y: 2, z: 4, core: 2. Of those that a mesh axis runs over, the one named last changes fastest.
Arguments:
- queries: bfloat16 [256, 8, 16, 128], P(('groups', 'prefix'), 'heads', 'sub'), parts along dimension 0, may hold values from -150 to 150
- prefix_keys: bfloat16 [16384, 8, 128], P(('groups', 'prefix'), 'heads'), parts along dimension 0, may hold values from -8 to 8
- prefix_values: bfloat16 [16384, 8, 128], P(('groups', 'prefix'), 'heads'), parts along dimension 0, may hold values from -9 to 9
- suffix_keys: bfloat16 [64, 1024, 8, 128], P(('groups', 'prefix'), None, 'heads'), parts along dimension 0, may hold values from -12 to 12
- suffix_values: bfloat16 [64, 1024, 8, 128], P(('groups', 'prefix'), None, 'heads'), parts along dimension 0, may hold values from -2 to 1
- accepted: int32 [64], P('groups'), parts along dimension 0, may hold values from 1 to 8, 128 in all
- cache_slot: int32 [64], P('groups'), parts along dimension 0, may hold values from 0 to 31, each once
- history: int32 [64], P('groups'), parts along dimension 0, may hold values from 128 to 1016
Outputs:
- attended: bfloat16 [256, 8, 16, 128], P(('groups', 'prefix'), 'heads', 'sub'), parts along dimension 0
The draws below stay inside these ranges and needn't reach their ends.
There are 2 independent parts, one for each index of `groups`. The reference program is written for one: setup_inputs(seed, part) draws one part's arguments, and reference() takes and returns one part's arrays. A program takes and returns all parts, laid end to end along the dimension named above; each array names one. Nothing has to cross between parts.
Inputs may be any that keep to these rules, and one draw needn't show every extreme that they name: `accepted`: the counts sum to 128, and the largest count is 8. `cache_slot`: each slot is named by exactly one request; slot s lies on index s // 8 of prefix, at place s % 8.
All inputs are finite; a program needn't handle non-finite values.
Results may differ from the reference program's by a relative error of at most 0.005.
Values may be sent and summed in bfloat16 or wider, within the bound.
A program may use at most 128 MiB of HBM per device.

```python
import math
import jax
import jax.numpy as jnp
import numpy as np
from jax import lax

KVH = 8
HD = 128
GROUP = 16
MOST = 8
SLEN = 1024
PLEN = 8192
REQUESTS = 32
TOKENS = 128


def shared_keys(key):
    keys_drawn = jax.random.normal(jax.random.fold_in(key, 7), (PLEN, KVH, HD), jnp.float32)
    return keys_drawn


def draw_prefix_keys(key, part):
    return shared_keys(key).astype(jnp.bfloat16)


def draw_queries(key, part):
    fresh = jax.random.normal(jax.random.fold_in(key, 9), (TOKENS, KVH, GROUP, HD), jnp.float32)
    return fresh.astype(jnp.bfloat16)


def draw_prefix_values(key, part):
    noise = jax.random.normal(jax.random.fold_in(key, 21), (PLEN, KVH, HD), jnp.float32)
    shifts = jax.random.uniform(jax.random.fold_in(key, 22), (PLEN // 32, KVH, HD), jnp.float32, -1.5, 1.5)
    shifts = jnp.repeat(shifts, 32, axis=0)
    return jnp.clip(noise + shifts, -9.0, 9.0).astype(jnp.bfloat16)


def set_ends(array, stream_key, low, high):
    longest = array.shape.index(max(array.shape))
    spots = []
    for shift in (0, 1):
        where = [jax.random.randint(jax.random.fold_in(stream_key, axis), (), 0, length) for axis, length in enumerate(array.shape)]
        where[longest] = (where[longest] + shift) % array.shape[longest]
        spots.append(tuple(where))
    return array.at[spots[0]].set(low).at[spots[1]].set(high)


def levels(stream_key, extent, split, low, high):
    def one(position, parts):
        steps = jax.random.uniform(jax.random.fold_in(jax.random.fold_in(stream_key, 6), position), (parts,), jnp.float32, low / len(split), high / len(split))
        return jnp.repeat(jnp.exp(steps), extent[position] // parts).reshape((-1,) + (1,) * (len(extent) - position - 1))

    loudness = one(*split[0])
    for cut in split[1:]:
        loudness = loudness * one(*cut)
    return loudness


def length_profile(amount, total, most, skew):
    loads = [(1 << 20) // math.isqrt(grade ** skew) + 1 for grade in range(2, amount + 1)]
    spare, counts = total - most - (amount - 1), [1] * (amount - 1)
    while spare > 0:
        candidates = [i for i in range(amount - 1) if counts[i] < most]
        whole, remaining = sum([loads[i] for i in candidates]), spare
        for i in candidates:
            extra = min(most - counts[i], max(1, remaining * loads[i] // whole), spare)
            counts[i] = counts[i] + extra
            spare = spare - extra
    return np.array([most] + counts)


def uneven(stream_key, amount, total, most, slope):
    if amount == 2:
        one = jax.random.randint(stream_key, (), max(1, total - most), min(most, total - 1) + 1)
        return jnp.stack([one, total - one])
    sizes = jnp.asarray(length_profile(amount, total, most, slope), jnp.int32)
    couples = (amount - 1) // 2
    source_of, taker = sizes[1:1 + 2 * couples:2], sizes[2:2 + 2 * couples:2]
    slack = jnp.minimum(source_of - 1, most - taker)
    passed = jax.random.randint(jax.random.fold_in(stream_key, 1), (couples,), 0, 1 << 20) % (slack + 1)
    sizes = sizes.at[1:1 + 2 * couples:2].set(source_of - passed).at[2:2 + 2 * couples:2].set(taker + passed)
    return sizes[jax.random.permutation(jax.random.fold_in(stream_key, 2), amount)]


def centred(key, extent, scale, bound, shards=(), kind=jnp.bfloat16):
    loudness = levels(key, extent, shards, -0.22, 0.18) if shards else 1.0
    array = jax.random.normal(key, extent, jnp.float32) * scale * loudness
    return jnp.minimum(jnp.maximum(array, -bound), bound).astype(kind)


def setup_inputs(seed: int = 0, part: int = 0) -> dict:
    key_list = jax.random.split(jax.random.key(seed), 9)
    part_keys = jax.random.split(jax.random.fold_in(key_list[8], part), 9)
    queries = draw_queries(jax.random.fold_in(jax.random.fold_in(key_list[8], part), 71), part)
    prefix_keys = draw_prefix_keys(jax.random.fold_in(jax.random.fold_in(key_list[8], part), 71), part)
    prefix_values = draw_prefix_values(jax.random.fold_in(jax.random.fold_in(key_list[8], part), 71), part)
    suffix_keys = centred(part_keys[3], (REQUESTS, SLEN, KVH, HD), 2.0, 12.0, ((0, 4), (2, 2)))
    suffix_values = jnp.clip(-2.0 + 3.0 * jax.random.uniform(part_keys[4], (REQUESTS, SLEN, KVH, HD), jnp.float32) ** levels(part_keys[4], (REQUESTS, SLEN, KVH, HD), ((0, 4), (2, 2)), -0.2, 0.2), -2.0, 1.0).astype(jnp.bfloat16)
    accepted = uneven(part_keys[5], REQUESTS, TOKENS, MOST, 2).astype(jnp.int32)
    cache_slot = jax.random.permutation(part_keys[6], REQUESTS).astype(jnp.int32)
    history = set_ends(jax.random.randint(part_keys[7], (REQUESTS,), SLEN // 8, SLEN - MOST + 1), jax.random.fold_in(part_keys[7], 1), SLEN // 8, SLEN - MOST).astype(jnp.int32)
    return dict(queries=queries, prefix_keys=prefix_keys, prefix_values=prefix_values, suffix_keys=suffix_keys, suffix_values=suffix_values, accepted=accepted, cache_slot=cache_slot, history=history)


negative = -1e+30

def reference(queries, prefix_keys, prefix_values, suffix_keys, suffix_values, accepted, cache_slot, history):
    scaling = 1.0 / math.sqrt(HD)
    request_ends = jnp.cumsum(accepted).astype(jnp.int32)
    starts = (request_ends - accepted).astype(jnp.int32)
    row_ids = jnp.arange(TOKENS, dtype=jnp.int32)
    request_of_row = lax.optimization_barrier(jnp.sum((row_ids[:, None] >= request_ends[None, :]).astype(jnp.int32), axis=1)).astype(jnp.int32)
    place_in = row_ids - starts[request_of_row]
    key_limit = (history[request_of_row] + place_in + 1).astype(jnp.int32)
    slot_of_row = cache_slot[request_of_row].astype(jnp.int32)
    key_span = jnp.arange(SLEN, dtype=jnp.int32)
    keys_wide = prefix_keys.astype(jnp.float32)
    values_wide = prefix_values.astype(jnp.float32)

    def one_block(inputs):
        query_block, slot_block, limit_block = inputs
        query_wide = query_block.astype(jnp.float32)
        own_keys = suffix_keys[slot_block].astype(jnp.float32)
        own_values = suffix_values[slot_block].astype(jnp.float32)
        prefix_score = jnp.einsum('rkgd,skd->rkgs', query_wide, keys_wide) * scaling
        suffix_score = jnp.einsum('rkgd,rskd->rkgs', query_wide, own_keys) * scaling
        allowed = (key_span[None, :] < limit_block[:, None])[:, None, None, :]
        top = jnp.maximum(lax.optimization_barrier(jnp.max(prefix_score, axis=-1)), lax.optimization_barrier(jnp.max(jnp.where(allowed, suffix_score, negative), axis=-1)))
        prefix_weight = jnp.exp(prefix_score - top[..., None])
        suffix_weight = jnp.where(allowed, jnp.exp(suffix_score - top[..., None]), 0.0)
        denominator = lax.optimization_barrier(jnp.sum(prefix_weight, axis=-1)) + lax.optimization_barrier(jnp.sum(suffix_weight, axis=-1))
        prefix_round = lax.optimization_barrier(prefix_weight.astype(jnp.bfloat16)).astype(jnp.float32)
        suffix_round = lax.optimization_barrier(suffix_weight.astype(jnp.bfloat16)).astype(jnp.float32)
        numerator = jnp.einsum('rkgs,skd->rkgd', prefix_round, values_wide)
        numerator = numerator + jnp.einsum('rkgs,rskd->rkgd', suffix_round, own_values)
        return (numerator / denominator[..., None]).astype(jnp.bfloat16)
    block_rows = 32
    blocked = queries.reshape(TOKENS // block_rows, block_rows, KVH, GROUP, HD)
    result = lax.map(one_block, (blocked, slot_of_row.reshape(-1, block_rows), key_limit.reshape(-1, block_rows)))
    return result.reshape(TOKENS, KVH, GROUP, HD)
```

```python
import functools
import math

import jax
import jax.numpy as jnp
from jax import lax
from jax.experimental import pallas as pl
from jax.experimental.pallas import tpu as pltpu
from jax.sharding import PartitionSpec as P


MOST = 8
NEG = -1e30
LOG2E = 1.4426950408889634


def nt_dot(a, b):
    return lax.dot_general(a, b, (((1,), (1,)), ((), ())), preferred_element_type=jnp.float32)


def block_kernel(
    meta,
    q_ref,
    k_ref,
    v_ref,
    sk_hbm,
    sv_hbm,
    o_ref,
    lse_ref,
    acc,
    top,
    den,
    kbuf,
    vbuf,
    hmask,
    tasks,
    sems,
    *,
    slots,
    chunk,
    scale,
):
    step = pl.program_id(0)
    heads = pl.num_programs(0)
    rows, kh, gs, hd = q_ref.shape
    first = meta[3 * slots]
    wide = chunk * kh
    window = MOST * kh * gs

    def copies(task, buf):
        slot = tasks[task, 0]
        base = tasks[task, 1] * wide
        src = pl.ds(pl.multiple_of(base, wide), wide)
        return (
            pltpu.make_async_copy(sk_hbm.at[slot, src], kbuf.at[buf], sems.at[0, buf]),
            pltpu.make_async_copy(sv_hbm.at[slot, src], vbuf.at[buf], sems.at[1, buf]),
        )

    @pl.when(step == 0)
    def _():
        total = jnp.int32(0)
        for slot in range(slots):
            begin = meta[slot]
            amount = meta[slots + slot]
            past = meta[2 * slots + slot]
            touches = (begin < first + rows) & (begin + amount > first)
            reach = jnp.where(touches, past + amount, 0)
            blocks = (reach + chunk - 1) // chunk

            def put(i, total, slot=slot):
                tasks[total, 0] = slot
                tasks[total, 1] = i
                return total + 1

            total = lax.fori_loop(0, blocks, put, total)
        tasks[tasks.shape[0] - 1, 0] = total

        @pl.when(total > 0)
        def _():
            for copy in copies(0, 0):
                copy.start()

        ids = lax.broadcasted_iota(jnp.int32, (wide, hd), 0)
        lanes = lax.broadcasted_iota(jnp.int32, (wide, hd), 1)
        hmask[...] = jnp.where(
            (lax.rem(ids, kh) != lanes) & (lanes < kh), 1.0, 0.0
        ).astype(jnp.bfloat16)

    q = q_ref[:, step].reshape(rows * gs, hd)
    s = nt_dot(q, k_ref[0])
    m = jnp.max(s, axis=1, keepdims=True) * scale
    p = jnp.exp2(s * scale - m).astype(jnp.bfloat16)
    v = v_ref[0]
    v_wide = jnp.concatenate([v, jnp.ones_like(v)], axis=1)
    pv = jnp.dot(p, v_wide, preferred_element_type=jnp.float32)
    acc[:, step] = pv[:, :hd].reshape(rows, gs, hd)
    den[:, step] = pv[:, hd:].reshape(rows, gs, hd)
    top[:, step] = jnp.broadcast_to(m, (rows * gs, hd)).reshape(rows, gs, hd)

    @pl.when(step == heads - 1)
    def _():
        total = tasks[tasks.shape[0] - 1, 0]
        i_row = lax.broadcasted_iota(jnp.int32, (window, 1), 0) // (kh * gs)
        pos = lax.broadcasted_iota(jnp.int32, (1, wide), 1) // kh
        i_full = lax.broadcasted_iota(jnp.int32, (window, hd), 0)
        lane = lax.broadcasted_iota(jnp.int32, (window, hd), 1)
        q_extra = jnp.where(lax.rem(i_full // gs, kh) == lane, NEG, 0.0).astype(jnp.bfloat16)

        def body(t, carry):
            buf = lax.rem(t, 2)

            @pl.when(t + 1 < total)
            def _():
                for copy in copies(t + 1, 1 - buf):
                    copy.start()

            slot = tasks[t, 0]
            base = tasks[t, 1] * chunk
            begin = meta[slot]
            amount = meta[slots + slot]
            past = meta[2 * slots + slot]
            start = jnp.clip(begin - first, 0, rows - MOST)
            place = i_row + (first + start - begin)
            limit = jnp.where((place >= 0) & (place < amount), past + place + 1, 0) - base
            rows_at = pl.ds(start, MOST)
            q_win = q_ref[rows_at].reshape(window, hd)
            q_wide = jnp.concatenate([q_win, q_extra], axis=1)
            for copy in copies(t, buf):
                copy.wait()
            k_wide = jnp.concatenate([kbuf[buf], hmask[...]], axis=1)
            s = nt_dot(q_wide, k_wide)
            s = jnp.where(pos < limit, s, NEG)
            old_top = top[rows_at].reshape(window, hd)
            m = jnp.maximum(old_top, jnp.max(s, axis=1, keepdims=True) * scale)
            p = jnp.exp2(s * scale - m[:, :1]).astype(jnp.bfloat16)
            v = vbuf[buf]
            pv = jnp.dot(
                p, jnp.concatenate([v, jnp.ones_like(v)], axis=1),
                preferred_element_type=jnp.float32,
            )
            factor = jnp.exp2(old_top - m)
            shape = (MOST, kh, gs, hd)
            top[rows_at] = m.reshape(shape)
            den[rows_at] = (den[rows_at].reshape(window, hd) * factor + pv[:, hd:]).reshape(shape)
            acc[rows_at] = (acc[rows_at].reshape(window, hd) * factor + pv[:, :hd]).reshape(shape)
            return carry

        lax.fori_loop(0, total, body, 0)
        d = den[...]
        o_ref[...] = (acc[...] / d).astype(o_ref.dtype)
        lse = (top[...] + jnp.log2(d)).reshape(rows * kh * gs // hd, hd, hd)
        eye = lax.broadcasted_iota(jnp.int32, (1, hd, hd), 1) == lax.broadcasted_iota(
            jnp.int32, (1, hd, hd), 2
        )
        lse_ref[...] = jnp.sum(jnp.where(eye, lse, 0.0), axis=1)


def block_part(q, home, table, kh_arr, vh_arr, sk, sv, out_dtype):
    rows, heads, gs, hd = q.shape
    plen = kh_arr.shape[1]
    slots, flat, _ = sk.shape
    slen = flat // heads
    chunk = min(slen, 256)
    meta = jnp.concatenate([table, (home * rows)[None].astype(jnp.int32)])
    most_tasks = slots * (slen // chunk)
    state = pltpu.VMEM((rows, heads, gs, hd), jnp.float32)
    kernel = functools.partial(
        block_kernel, slots=slots, chunk=chunk, scale=LOG2E / math.sqrt(hd)
    )
    return pl.pallas_call(
        kernel,
        grid_spec=pltpu.PrefetchScalarGridSpec(
            num_scalar_prefetch=1,
            grid=(heads,),
            in_specs=[
                pl.BlockSpec((rows, heads, gs, hd), lambda h, m: (0, 0, 0, 0)),
                pl.BlockSpec((1, plen, hd), lambda h, m: (h, 0, 0)),
                pl.BlockSpec((1, plen, hd), lambda h, m: (h, 0, 0)),
                pl.BlockSpec(memory_space=pltpu.HBM),
                pl.BlockSpec(memory_space=pltpu.HBM),
            ],
            out_specs=[
                pl.BlockSpec((rows, heads, gs, hd), lambda h, m: (0, 0, 0, 0)),
                pl.BlockSpec((rows * heads * gs // hd, hd), lambda h, m: (0, 0)),
            ],
            scratch_shapes=[
                state,
                state,
                state,
                pltpu.VMEM((2, chunk * heads, hd), jnp.bfloat16),
                pltpu.VMEM((2, chunk * heads, hd), jnp.bfloat16),
                pltpu.VMEM((chunk * heads, hd), jnp.bfloat16),
                pltpu.SMEM((most_tasks + 1, 2), jnp.int32),
                pltpu.SemaphoreType.DMA((2, 2)),
            ],
        ),
        out_shape=[
            jax.ShapeDtypeStruct(q.shape, out_dtype),
            jax.ShapeDtypeStruct((rows * heads * gs // hd, hd), jnp.float32),
        ],
        cost_estimate=pl.CostEstimate(
            flops=8 * rows * heads * gs * hd * plen,
            bytes_accessed=4 * plen * heads * hd + 4 * slots * flat * hd // 4,
            transcendentals=rows * heads * gs * plen,
        ),
        compiler_params=pltpu.CompilerParams(vmem_limit_bytes=48 * 1024 * 1024),
    )(meta, q, kh_arr, vh_arr, sk, sv)


def merge_kernel(*refs, count):
    outs = refs[:count]
    lses = refs[count : 2 * count]
    result = refs[2 * count]
    rows, heads, gs, hd = result.shape
    total_rows = rows * heads * gs
    groups = total_rows // hd
    highest = lses[0][...]
    for ref in lses[1:]:
        highest = jnp.maximum(highest, ref[...])
    weights = [jnp.exp2(ref[...] - highest) for ref in lses]
    total = sum(weights)
    eye = lax.broadcasted_iota(jnp.int32, (1, hd, hd), 1) == lax.broadcasted_iota(
        jnp.int32, (1, hd, hd), 2
    )
    summed = jnp.zeros((total_rows, hd), jnp.float32)
    for ref, weight in zip(outs, weights):
        lanes = jnp.broadcast_to((weight / total)[:, None, :], (groups, hd, hd))
        column = jnp.sum(jnp.where(eye, lanes, 0.0), axis=2, keepdims=True)
        column = column.reshape(total_rows, 1)
        summed = summed + ref[...].astype(jnp.float32).reshape(total_rows, hd) * column
    result[...] = summed.astype(result.dtype).reshape(result.shape)


def merged(outs, lses, shape):
    return pl.pallas_call(
        functools.partial(merge_kernel, count=len(outs)),
        out_shape=jax.ShapeDtypeStruct(shape, jnp.bfloat16),
        compiler_params=pltpu.CompilerParams(vmem_limit_bytes=48 * 1024 * 1024),
    )(*outs, *lses)


def owned_requests(accepted, cache_slot, history, owner_index, held_slots):
    request_ends = jnp.cumsum(accepted)
    starts = request_ends - accepted
    wanted = owner_index * held_slots + jnp.arange(held_slots, dtype=jnp.int32)
    matches = (cache_slot[None, :] == wanted[:, None]).astype(jnp.int32)
    data = jnp.stack([starts, accepted, history])
    return jnp.sum(matches[None] * data[:, None, :], axis=2).reshape(-1)


def shifted(value, steps):
    count = lax.axis_size("prefix")
    pairs = [(source, (source + steps) % count) for source in range(count)]
    return lax.ppermute(value, "prefix", pairs)


def local(
    queries, prefix_keys, prefix_values, suffix_keys, suffix_values, accepted, cache_slot, history
):
    owner = lax.axis_index("prefix")
    parties = lax.axis_size("prefix")
    slots, slen, heads, hd = suffix_keys.shape
    arrived = [queries] + [shifted(queries, step) for step in range(1, parties)]
    table = owned_requests(accepted, cache_slot, history, owner, slots)
    kh = prefix_keys.transpose(1, 0, 2)
    vh = prefix_values.transpose(1, 0, 2)
    sk = suffix_keys.reshape(slots, slen * heads, hd)
    sv = suffix_values.reshape(slots, slen * heads, hd)
    outs, lses = [], []
    for step in range(parties):
        home = (owner - step) % parties
        dtype = jnp.float32 if step == 0 else jnp.bfloat16
        out, lse = block_part(arrived[step], home, table, kh, vh, sk, sv, dtype)
        if step:
            out, lse = shifted(out, -step), shifted(lse, -step)
        outs.append(out)
        lses.append(lse)
    return merged(outs, lses, queries.shape)


def solution(mesh):
    in_specs = (
        P(("groups", "prefix"), "heads", "sub", None),
        P(("groups", "prefix"), "heads", None),
        P(("groups", "prefix"), "heads", None),
        P(("groups", "prefix"), None, "heads", None),
        P(("groups", "prefix"), None, "heads", None),
        P("groups"),
        P("groups"),
        P("groups"),
    )
    out_specs = P(("groups", "prefix"), "heads", "sub", None)
    return jax.shard_map(local, mesh=mesh, in_specs=in_specs, out_specs=out_specs, check_vma=False)
```

```python
import functools
import math

import jax
import jax.numpy as jnp
from jax import lax
from jax.experimental import pallas as pl
from jax.experimental.pallas import tpu as pltpu
from jax.sharding import PartitionSpec as P


MOST = 8
NEG = -1e30
LOG2E = 1.4426950408889634


def nt_dot(a, b):
    return lax.dot_general(a, b, (((1,), (1,)), ((), ())), preferred_element_type=jnp.float32)


def split_three(x):
    high = x.astype(jnp.bfloat16)
    rest = x - high.astype(jnp.float32)
    middle = rest.astype(jnp.bfloat16)
    low = (rest - middle.astype(jnp.float32)).astype(jnp.bfloat16)
    return high, middle, low


def block_kernel(
    meta, q_ref, k_ref, v_ref, sk_hbm, sv_hbm, *rest, slots, chunk, scale, home_block
):
    if home_block:
        o_ref, lse_ref, acc, top, den, kbuf, vbuf, tasks, sems = rest
    else:
        o_ref, acc, top, den, kbuf, vbuf, tasks, sems = rest
    rows, kh, gs, hd = q_ref.shape
    plen = k_ref.shape[1]
    first = meta[3 * slots]
    wide = chunk * kh
    window = MOST * gs
    depth = kbuf.shape[0]

    def copies(task, buf):
        slot = tasks[task, 0]
        base = tasks[task, 1] * wide
        src = pl.ds(pl.multiple_of(base, wide), wide)
        return (
            pltpu.make_async_copy(sk_hbm.at[slot, src], kbuf.at[buf], sems.at[0, buf]),
            pltpu.make_async_copy(sv_hbm.at[slot, src], vbuf.at[buf], sems.at[1, buf]),
        )

    total = jnp.int32(0)
    for slot in range(slots):
        begin = meta[slot]
        amount = meta[slots + slot]
        past = meta[2 * slots + slot]
        touches = (begin < first + rows) & (begin + amount > first)
        reach = jnp.where(touches, past + amount, 0)
        blocks = (reach + chunk - 1) // chunk

        def put(i, count, slot=slot):
            tasks[count, 0] = slot
            tasks[count, 1] = i
            return count + 1

        total = lax.fori_loop(0, blocks, put, total)

    for ahead in range(depth - 1):

        @pl.when(ahead < total)
        def _(ahead=ahead):
            for copy in copies(ahead, ahead):
                copy.start()

    part = min(plen, 1024)
    pieces = plen // part
    stages = [(h, c) for h in range(kh) for c in range(pieces)]

    def score(stage):
        h, c = stage
        q = q_ref[:, h].reshape(rows * gs, hd)
        return nt_dot(q, k_ref[h, pl.ds(c * part, part), :])

    ready = score(stages[0])
    held = []
    for index, (h, c) in enumerate(stages):
        s = ready
        if index + 1 < len(stages):
            ready = score(stages[index + 1])
        m = jnp.max(s, axis=1, keepdims=True) * scale
        p = jnp.exp2(s * scale - m).astype(jnp.bfloat16)
        v = v_ref[h, pl.ds(c * part, part), :]
        pv = jnp.dot(
            p, jnp.concatenate([v, jnp.ones_like(v)], axis=1),
            preferred_element_type=jnp.float32,
        )
        held.append((m, pv))
        if c == pieces - 1:
            m, pv = held[0]
            for m_more, pv_more in held[1:]:
                joined = jnp.maximum(m, m_more)
                pv = pv * jnp.exp2(m - joined) + pv_more * jnp.exp2(m_more - joined)
                m = joined
            held = []
            acc[:, h] = pv[:, :hd].reshape(rows, gs, hd)
            den[:, h] = pv[:, hd:].reshape(rows, gs, hd)
            top[:, h] = jnp.broadcast_to(m, (rows * gs, hd)).reshape(rows, gs, hd)

    unit = 256 if wide % 256 == 0 else wide
    per = unit // kh
    i_at = lax.broadcasted_iota(jnp.int32, (unit, unit), 0)
    j_at = lax.broadcasted_iota(jnp.int32, (unit, unit), 1)
    sort = jnp.where(lax.rem(i_at, per) * kh + i_at // per == j_at, 1.0, 0.0)
    sort = sort.astype(jnp.bfloat16)
    i_row = lax.broadcasted_iota(jnp.int32, (window, 1), 0) // gs
    pos = lax.broadcasted_iota(jnp.int32, (1, chunk), 1)

    def by_head(ref, buf):
        groups = [
            jnp.dot(
                sort, ref[buf, pl.ds(g * unit, unit), :], preferred_element_type=jnp.float32
            ).astype(jnp.bfloat16)
            for g in range(wide // unit)
        ]
        return [
            jnp.concatenate([group[h * per : (h + 1) * per] for group in groups], axis=0)
            for h in range(kh)
        ]

    def body(t, carry):
        buf = lax.rem(t, depth)

        @pl.when(t + depth - 1 < total)
        def _():
            for copy in copies(t + depth - 1, lax.rem(t + depth - 1, depth)):
                copy.start()

        slot = tasks[t, 0]
        base = tasks[t, 1] * chunk
        begin = meta[slot]
        amount = meta[slots + slot]
        past = meta[2 * slots + slot]
        start = jnp.clip(begin - first, 0, rows - MOST)
        place = i_row + (first + start - begin)
        limit = jnp.where((place >= 0) & (place < amount), past + place + 1, 0) - base
        allowed = pos < limit
        rows_at = pl.ds(start, MOST)
        for copy in copies(t, buf):
            copy.wait()
        keys = by_head(kbuf, buf)
        scores = [
            nt_dot(q_ref[rows_at, h].reshape(window, hd), keys[h]) for h in range(kh)
        ]
        values = by_head(vbuf, buf)
        shape = (MOST, gs, hd)
        for h in range(kh):
            s = jnp.where(allowed, scores[h], NEG)
            old_top = top[rows_at, h].reshape(window, hd)
            m = jnp.maximum(old_top, jnp.max(s, axis=1, keepdims=True) * scale)
            p = jnp.exp2(s * scale - m[:, :1]).astype(jnp.bfloat16)
            v = values[h]
            pv = jnp.dot(
                p, jnp.concatenate([v, jnp.ones_like(v)], axis=1),
                preferred_element_type=jnp.float32,
            )
            factor = jnp.exp2(old_top - m)
            top[rows_at, h] = m.reshape(shape)
            den[rows_at, h] = (
                den[rows_at, h].reshape(window, hd) * factor + pv[:, hd:]
            ).reshape(shape)
            acc[rows_at, h] = (
                acc[rows_at, h].reshape(window, hd) * factor + pv[:, :hd]
            ).reshape(shape)
        return carry

    lax.fori_loop(0, total, body, 0)
    d = den[...]
    out = (acc[...] / d).astype(o_ref.dtype)
    lse = (top[...] + jnp.log2(d)).reshape(rows * kh * gs // hd, hd, hd)
    eye = lax.broadcasted_iota(jnp.int32, (1, hd, hd), 1) == lax.broadcasted_iota(
        jnp.int32, (1, hd, hd), 2
    )
    lse = jnp.sum(jnp.where(eye, lse, 0.0), axis=1)
    if home_block:
        o_ref[...] = out
        lse_ref[...] = lse
    else:
        tiles = -(-lse.shape[0] // gs)
        padding = tiles * gs - lse.shape[0]
        if padding:
            lse = jnp.concatenate([lse, jnp.zeros((padding, hd), lse.dtype)], axis=0)
        o_ref[pl.ds(0, rows)] = out
        pieces = []
        for piece in split_three(lse):
            piece = piece.reshape(tiles, gs, hd)
            pieces.append(piece)
        flat = jnp.concatenate(pieces, axis=0)
        spare = (o_ref.shape[0] - rows) * kh - flat.shape[0]
        if spare:
            flat = jnp.concatenate([flat, jnp.zeros((spare, gs, hd), flat.dtype)], axis=0)
        o_ref[pl.ds(rows, o_ref.shape[0] - rows)] = flat.reshape(
            o_ref.shape[0] - rows, kh, gs, hd
        )


def stat_rows(shape):
    rows, heads, gs, hd = shape
    tiles = 3 * -(-(rows * heads * gs // hd) // gs)
    return -(-tiles // heads)


def block_part(q, home, table, kh_arr, vh_arr, sk, sv, home_block):
    rows, heads, gs, hd = q.shape
    plen = kh_arr.shape[1]
    slots, flat, _ = sk.shape
    slen = flat // heads
    chunk = min(slen, 256)
    meta = jnp.concatenate([table, (home * rows)[None].astype(jnp.int32)])
    most_tasks = slots * (slen // chunk)
    state = pltpu.VMEM((rows, heads, gs, hd), jnp.float32)
    kernel = functools.partial(
        block_kernel,
        slots=slots,
        chunk=chunk,
        scale=LOG2E / math.sqrt(hd),
        home_block=home_block,
    )
    if home_block:
        out_shape = [
            jax.ShapeDtypeStruct(q.shape, jnp.float32),
            jax.ShapeDtypeStruct((rows * heads * gs // hd, hd), jnp.float32),
        ]
    else:
        out_shape = [
            jax.ShapeDtypeStruct((rows + stat_rows(q.shape), heads, gs, hd), jnp.bfloat16)
        ]
    vmem = pl.BlockSpec(memory_space=pltpu.VMEM)
    hbm = pl.BlockSpec(memory_space=pltpu.HBM)
    return pl.pallas_call(
        kernel,
        in_specs=[pl.BlockSpec(memory_space=pltpu.SMEM), vmem, vmem, vmem, hbm, hbm],
        out_specs=[vmem] * len(out_shape),
        scratch_shapes=[
            state,
            state,
            state,
            pltpu.VMEM((4, chunk * heads, hd), jnp.bfloat16),
            pltpu.VMEM((4, chunk * heads, hd), jnp.bfloat16),
            pltpu.SMEM((most_tasks, 2), jnp.int32),
            pltpu.SemaphoreType.DMA((2, 4)),
        ],
        out_shape=out_shape,
        cost_estimate=pl.CostEstimate(
            flops=8 * rows * heads * gs * hd * plen,
            bytes_accessed=4 * plen * heads * hd + 4 * slots * flat * hd // 4,
            transcendentals=rows * heads * gs * plen,
        ),
        compiler_params=pltpu.CompilerParams(vmem_limit_bytes=40 * 1024 * 1024),
    )(meta, q, kh_arr, vh_arr, sk, sv)


def merge_kernel(*refs):
    own, own_lse = refs[0], refs[1]
    others = refs[2:-1]
    result = refs[-1]
    rows, heads, gs, hd = result.shape
    total_rows = rows * heads * gs
    groups = total_rows // hd
    tiles = -(-groups // gs)
    lses = [own_lse[...]]
    for ref in others:
        flat = ref[pl.ds(rows, ref.shape[0] - rows)].astype(jnp.float32)
        flat = flat.reshape((ref.shape[0] - rows) * heads, gs, hd)
        high, middle, low = (flat[i * tiles : (i + 1) * tiles] for i in range(3))
        lses.append((high + middle + low).reshape(tiles * gs, hd)[:groups])
    highest = lses[0]
    for lse in lses[1:]:
        highest = jnp.maximum(highest, lse)
    weights = [jnp.exp2(lse - highest) for lse in lses]
    total = sum(weights)
    eye = lax.broadcasted_iota(jnp.int32, (1, hd, hd), 1) == lax.broadcasted_iota(
        jnp.int32, (1, hd, hd), 2
    )
    summed = jnp.zeros((total_rows, hd), jnp.float32)
    for ref, weight in zip((own,) + tuple(others), weights):
        lanes = jnp.broadcast_to((weight / total)[:, None, :], (groups, hd, hd))
        column = jnp.sum(jnp.where(eye, lanes, 0.0), axis=2, keepdims=True)
        column = column.reshape(total_rows, 1)
        block = ref[pl.ds(0, rows)].astype(jnp.float32).reshape(total_rows, hd)
        summed = summed + block * column
    result[...] = summed.astype(result.dtype).reshape(result.shape)


def merged(own, own_lse, others, shape):
    return pl.pallas_call(
        merge_kernel,
        out_shape=jax.ShapeDtypeStruct(shape, jnp.bfloat16),
        compiler_params=pltpu.CompilerParams(vmem_limit_bytes=40 * 1024 * 1024),
    )(own, own_lse, *others)


def owned_requests(accepted, cache_slot, history, owner_index, held_slots):
    request_ends = jnp.cumsum(accepted)
    starts = request_ends - accepted
    wanted = owner_index * held_slots + jnp.arange(held_slots, dtype=jnp.int32)
    matches = (cache_slot[None, :] == wanted[:, None]).astype(jnp.int32)
    data = jnp.stack([starts, accepted, history])
    return jnp.sum(matches[None] * data[:, None, :], axis=2).reshape(-1)


def shifted(value, steps):
    count = lax.axis_size("prefix")
    pairs = [(source, (source + steps) % count) for source in range(count)]
    return lax.ppermute(value, "prefix", pairs)


def local(
    queries, prefix_keys, prefix_values, suffix_keys, suffix_values, accepted, cache_slot, history
):
    owner = lax.axis_index("prefix")
    parties = lax.axis_size("prefix")
    slots, slen, heads, hd = suffix_keys.shape
    arrived = [queries] + [shifted(queries, step) for step in range(1, parties)]
    table = owned_requests(accepted, cache_slot, history, owner, slots)
    kh = prefix_keys.transpose(1, 0, 2)
    vh = prefix_values.transpose(1, 0, 2)
    sk = suffix_keys.reshape(slots, slen * heads, hd)
    sv = suffix_values.reshape(slots, slen * heads, hd)
    others = []
    for step in range(1, parties):
        home = (owner - step) % parties
        (out,) = block_part(arrived[step], home, table, kh, vh, sk, sv, False)
        others.append(shifted(out, -step))
    own, own_lse = block_part(queries, owner, table, kh, vh, sk, sv, True)
    return merged(own, own_lse, others, queries.shape)


def solution(mesh):
    in_specs = (
        P(("groups", "prefix"), "heads", "sub", None),
        P(("groups", "prefix"), "heads", None),
        P(("groups", "prefix"), "heads", None),
        P(("groups", "prefix"), None, "heads", None),
        P(("groups", "prefix"), None, "heads", None),
        P("groups"),
        P("groups"),
        P("groups"),
    )
    out_specs = P(("groups", "prefix"), "heads", "sub", None)
    return jax.shard_map(local, mesh=mesh, in_specs=in_specs, out_specs=out_specs, check_vma=False)
```

```python
import functools
import math

import jax
import jax.numpy as jnp
from jax import lax
from jax.experimental import pallas as pl
from jax.experimental.pallas import tpu as pltpu
from jax.sharding import PartitionSpec as P


MOST = 8
NEG = -1e30
UNSEEN = -1e20
LOG2E = 1.4426950408889634


def nt_dot(a, b):
    return lax.dot_general(a, b, (((1,), (1,)), ((), ())), preferred_element_type=jnp.float32)


def split_three(x):
    high = x.astype(jnp.bfloat16)
    rest = x - high.astype(jnp.float32)
    middle = rest.astype(jnp.bfloat16)
    low = (rest - middle.astype(jnp.float32)).astype(jnp.bfloat16)
    return high, middle, low


def suffix_kernel(
    meta, q_ref, sk_hbm, sv_hbm, acc, den, top, kbuf, vbuf, tasks, sems, *, slots, chunk, scale
):
    parties, rows, kh, gs, hd = q_ref.shape
    owner = meta[3 * slots]
    wide = chunk * kh
    window = MOST * gs
    depth = kbuf.shape[0]

    def copies(task, buf):
        slot = tasks[task, 0]
        base = tasks[task, 1] * wide
        src = pl.ds(pl.multiple_of(base, wide), wide)
        return (
            pltpu.make_async_copy(sk_hbm.at[slot, src], kbuf.at[buf], sems.at[0, buf]),
            pltpu.make_async_copy(sv_hbm.at[slot, src], vbuf.at[buf], sems.at[1, buf]),
        )

    total = jnp.int32(0)
    for slot in range(slots):
        begin = meta[slot]
        amount = meta[slots + slot]
        past = meta[2 * slots + slot]
        blocks = (past + amount + chunk - 1) // chunk
        home = begin // rows
        last_home = (begin + amount - 1) // rows
        for side in range(2):
            place = home if side == 0 else last_home
            wanted = blocks if side == 0 else jnp.where(last_home == home, 0, blocks)

            def put(i, count, slot=slot, place=place):
                tasks[count, 0] = slot
                tasks[count, 1] = i
                tasks[count, 2] = place
                return count + 1

            total = lax.fori_loop(0, wanted, put, total)

    for ahead in range(depth - 1):

        @pl.when(ahead < total)
        def _(ahead=ahead):
            for copy in copies(ahead, ahead):
                copy.start()

    acc[...] = jnp.zeros(acc.shape, acc.dtype)
    den[...] = jnp.zeros(den.shape, den.dtype)
    top[...] = jnp.full(top.shape, UNSEEN, top.dtype)

    unit = 256 if wide % 256 == 0 else wide
    per = unit // kh
    i_at = lax.broadcasted_iota(jnp.int32, (unit, unit), 0)
    j_at = lax.broadcasted_iota(jnp.int32, (unit, unit), 1)
    sort = jnp.where(lax.rem(i_at, per) * kh + i_at // per == j_at, 1.0, 0.0)
    sort = sort.astype(jnp.bfloat16)
    i_row = lax.broadcasted_iota(jnp.int32, (window, 1), 0) // gs
    pos = lax.broadcasted_iota(jnp.int32, (1, chunk), 1)

    def by_head(ref, buf):
        groups = [
            jnp.dot(
                sort, ref[buf, pl.ds(g * unit, unit), :], preferred_element_type=jnp.float32
            ).astype(jnp.bfloat16)
            for g in range(wide // unit)
        ]
        return [
            jnp.concatenate([group[h * per : (h + 1) * per] for group in groups], axis=0)
            for h in range(kh)
        ]

    def body(t, carry):
        buf = lax.rem(t, depth)

        @pl.when(t + depth - 1 < total)
        def _():
            for copy in copies(t + depth - 1, lax.rem(t + depth - 1, depth)):
                copy.start()

        slot = tasks[t, 0]
        base = tasks[t, 1] * chunk
        home = tasks[t, 2]
        first = home * rows
        at = lax.rem(owner - home - 1 + 2 * parties, parties)
        begin = meta[slot]
        amount = meta[slots + slot]
        past = meta[2 * slots + slot]
        start = jnp.clip(begin - first, 0, rows - MOST)
        place = i_row + (first + start - begin)
        limit = jnp.where((place >= 0) & (place < amount), past + place + 1, 0) - base
        allowed = pos < limit
        rows_at = pl.ds(start, MOST)
        for copy in copies(t, buf):
            copy.wait()
        keys = by_head(kbuf, buf)
        scores = [
            nt_dot(q_ref[at, rows_at, h].reshape(window, hd), keys[h]) for h in range(kh)
        ]
        values = by_head(vbuf, buf)
        shape = (MOST, gs, hd)
        for h in range(kh):
            s = jnp.where(allowed, scores[h], NEG)
            old_top = top[at, rows_at, h].reshape(window, hd)
            m = jnp.maximum(old_top, jnp.max(s, axis=1, keepdims=True) * scale)
            p = jnp.exp2(s * scale - m[:, :1]).astype(jnp.bfloat16)
            v = values[h]
            pv = jnp.dot(
                p, jnp.concatenate([v, jnp.ones_like(v)], axis=1),
                preferred_element_type=jnp.float32,
            )
            factor = jnp.exp2(old_top - m)
            top[at, rows_at, h] = m.reshape(shape)
            den[at, rows_at, h] = (
                den[at, rows_at, h].reshape(window, hd) * factor + pv[:, hd:]
            ).reshape(shape)
            acc[at, rows_at, h] = (
                acc[at, rows_at, h].reshape(window, hd) * factor + pv[:, :hd]
            ).reshape(shape)
        return carry

    lax.fori_loop(0, total, body, 0)


def suffix_state(q_all, meta, sk, sv):
    parties, rows, heads, gs, hd = q_all.shape
    slots, flat, _ = sk.shape
    slen = flat // heads
    chunk = min(slen, 256)
    vmem = pl.BlockSpec(memory_space=pltpu.VMEM)
    hbm = pl.BlockSpec(memory_space=pltpu.HBM)
    return pl.pallas_call(
        functools.partial(
            suffix_kernel, slots=slots, chunk=chunk, scale=LOG2E / math.sqrt(hd)
        ),
        in_specs=[pl.BlockSpec(memory_space=pltpu.SMEM), vmem, hbm, hbm],
        out_specs=[vmem] * 3,
        scratch_shapes=[
            pltpu.VMEM((4, chunk * heads, hd), jnp.bfloat16),
            pltpu.VMEM((4, chunk * heads, hd), jnp.bfloat16),
            pltpu.SMEM((2 * slots * (slen // chunk), 3), jnp.int32),
            pltpu.SemaphoreType.DMA((2, 4)),
        ],
        out_shape=[jax.ShapeDtypeStruct(q_all.shape, jnp.float32)] * 3,
        cost_estimate=pl.CostEstimate(
            flops=8 * MOST * heads * gs * hd * slots * slen,
            bytes_accessed=4 * slots * flat * hd,
            transcendentals=MOST * heads * gs * slots * slen,
        ),
        compiler_params=pltpu.CompilerParams(vmem_limit_bytes=24 * 1024 * 1024),
    )(meta, q_all, sk, sv)


def diagonal(hd):
    return lax.broadcasted_iota(jnp.int32, (1, hd, hd), 1) == lax.broadcasted_iota(
        jnp.int32, (1, hd, hd), 2
    )


def exchange_kernel(
    q_ref, k_ref, v_ref, acc_in, den_in, top_in, result, sent, got, own, lse_at, send_sems,
    recv_sems, *, scale
):
    parties, rows, kh, gs, hd = q_ref.shape
    plen = k_ref.shape[1]
    me = lax.axis_index("prefix")
    mesh_id = pl.DeviceIdType.MESH
    if parties > 1:
        barrier = pltpu.get_barrier_semaphore()
        for step in range(1, parties):
            pl.semaphore_signal(
                barrier,
                inc=1,
                device_id={"prefix": lax.rem(me + step, parties)},
                device_id_type=mesh_id,
            )
        pl.semaphore_wait(barrier, parties - 1)

    part = min(plen, 1024)
    pieces = plen // part
    stages = [(h, c) for h in range(kh) for c in range(pieces)]
    total_rows = rows * kh * gs
    groups = total_rows // hd
    tiles = -(-groups // gs)

    def block(at, put_out):
        def score(stage):
            h, c = stage
            q = q_ref[at, :, h].reshape(rows * gs, hd)
            return nt_dot(q, k_ref[h, pl.ds(c * part, part), :])

        ready = score(stages[0])
        held = []
        for index, (h, c) in enumerate(stages):
            s = ready
            if index + 1 < len(stages):
                ready = score(stages[index + 1])
            m = jnp.max(s, axis=1, keepdims=True) * scale
            p = jnp.exp2(s * scale - m).astype(jnp.bfloat16)
            v = v_ref[h, pl.ds(c * part, part), :]
            pv = jnp.dot(
                p, jnp.concatenate([v, jnp.ones_like(v)], axis=1),
                preferred_element_type=jnp.float32,
            )
            held.append((m, pv))
            if c == pieces - 1:
                t = top_in[at, :, h].reshape(rows * gs, hd)
                joined = t
                for m, _ in held:
                    joined = jnp.maximum(joined, m)
                factor = jnp.exp2(t - joined)
                d = den_in[at, :, h].reshape(rows * gs, hd) * factor
                o = acc_in[at, :, h].reshape(rows * gs, hd) * factor
                for m, pv in held:
                    factor = jnp.exp2(m - joined)
                    d = d + pv[:, hd:] * factor
                    o = o + pv[:, :hd] * factor
                held = []
                put_out(h, (o / d).reshape(rows, gs, hd))
                lse_at[:, h] = (joined + jnp.log2(d)).reshape(rows, gs, hd)
        lse = lse_at[...].reshape(groups, hd, hd)
        return jnp.sum(jnp.where(diagonal(hd), lse, 0.0), axis=1)

    def copy_to(at):
        return pltpu.make_async_remote_copy(
            src_ref=sent.at[at],
            dst_ref=got.at[at],
            send_sem=send_sems.at[at],
            recv_sem=recv_sems.at[at],
            device_id={"prefix": lax.rem(me - at - 1 + parties, parties)},
            device_id_type=mesh_id,
        )

    def remote(at, carry):
        def put_out(h, value):
            sent[at, pl.ds(0, rows), h] = value.astype(sent.dtype)

        lse = block(at, put_out)
        padding = tiles * gs - groups
        if padding:
            lse = jnp.concatenate([lse, jnp.zeros((padding, hd), lse.dtype)], axis=0)
        parts = [piece.reshape(tiles, gs, hd) for piece in split_three(lse)]
        flat = jnp.concatenate(parts, axis=0)
        extra = sent.shape[1] - rows
        spare = extra * kh - flat.shape[0]
        if spare:
            flat = jnp.concatenate([flat, jnp.zeros((spare, gs, hd), flat.dtype)], axis=0)
        sent[at, pl.ds(rows, extra)] = flat.reshape(extra, kh, gs, hd)
        copy_to(at).start()
        return carry

    lax.fori_loop(0, parties - 1, remote, 0)

    def keep(h, value):
        own[:, h] = value

    lses = [block(parties - 1, keep)]
    for at in range(parties - 1):
        copy_to(at).wait()
        extra = got.shape[1] - rows
        flat = got[at, pl.ds(rows, extra)].astype(jnp.float32).reshape(extra * kh, gs, hd)
        high, middle, low = (flat[i * tiles : (i + 1) * tiles] for i in range(3))
        lses.append((high + middle + low).reshape(tiles * gs, hd)[:groups])
    highest = lses[0]
    for lse in lses[1:]:
        highest = jnp.maximum(highest, lse)
    weights = [jnp.exp2(lse - highest) for lse in lses]
    total = sum(weights)
    summed = jnp.zeros((total_rows, hd), jnp.float32)
    for index, weight in enumerate(weights):
        lanes = jnp.broadcast_to((weight / total)[:, None, :], (groups, hd, hd))
        column = jnp.sum(jnp.where(diagonal(hd), lanes, 0.0), axis=2, keepdims=True)
        column = column.reshape(total_rows, 1)
        part_out = own[...] if index == 0 else got[index - 1, pl.ds(0, rows)]
        summed = summed + part_out.astype(jnp.float32).reshape(total_rows, hd) * column
    result[...] = summed.astype(result.dtype).reshape(result.shape)


def stat_rows(shape):
    rows, heads, gs, hd = shape
    tiles = 3 * -(-(rows * heads * gs // hd) // gs)
    return -(-tiles // heads)


def exchanged(q_all, kh_arr, vh_arr, state):
    parties, rows, heads, gs, hd = q_all.shape
    travel = (max(parties - 1, 1), rows + stat_rows(q_all.shape[1:]), heads, gs, hd)
    block = pltpu.VMEM((rows, heads, gs, hd), jnp.float32)
    vmem = pl.BlockSpec(memory_space=pltpu.VMEM)
    return pl.pallas_call(
        functools.partial(exchange_kernel, scale=LOG2E / math.sqrt(hd)),
        in_specs=[vmem] * 6,
        out_specs=vmem,
        scratch_shapes=[
            pltpu.VMEM(travel, jnp.bfloat16),
            pltpu.VMEM(travel, jnp.bfloat16),
            block,
            block,
            pltpu.SemaphoreType.DMA((travel[0],)),
            pltpu.SemaphoreType.DMA((travel[0],)),
        ],
        out_shape=jax.ShapeDtypeStruct(q_all.shape[1:], jnp.bfloat16),
        compiler_params=pltpu.CompilerParams(
            vmem_limit_bytes=32 * 1024 * 1024, collective_id=0, has_side_effects=True
        ),
    )(q_all, kh_arr, vh_arr, *state)


def owned_requests(accepted, cache_slot, history, owner_index, held_slots):
    request_ends = jnp.cumsum(accepted)
    starts = request_ends - accepted
    wanted = owner_index * held_slots + jnp.arange(held_slots, dtype=jnp.int32)
    matches = (cache_slot[None, :] == wanted[:, None]).astype(jnp.int32)
    data = jnp.stack([starts, accepted, history])
    return jnp.sum(matches[None] * data[:, None, :], axis=2).reshape(-1)


def shifted(value, steps):
    count = lax.axis_size("prefix")
    pairs = [(source, (source + steps) % count) for source in range(count)]
    return lax.ppermute(value, "prefix", pairs)


def local(
    queries, prefix_keys, prefix_values, suffix_keys, suffix_values, accepted, cache_slot, history
):
    owner = lax.axis_index("prefix")
    parties = lax.axis_size("prefix")
    slots, slen, heads, hd = suffix_keys.shape
    arrived = [shifted(queries, step) for step in range(1, parties)] + [queries]
    table = owned_requests(accepted, cache_slot, history, owner, slots)
    meta = jnp.concatenate([table, owner[None].astype(jnp.int32)])
    kh = prefix_keys.transpose(1, 0, 2)
    vh = prefix_values.transpose(1, 0, 2)
    sk = suffix_keys.reshape(slots, slen * heads, hd)
    sv = suffix_values.reshape(slots, slen * heads, hd)
    q_all = jnp.stack(arrived)
    state = suffix_state(q_all, meta, sk, sv)
    return exchanged(q_all, kh, vh, state)


def solution(mesh):
    in_specs = (
        P(("groups", "prefix"), "heads", "sub", None),
        P(("groups", "prefix"), "heads", None),
        P(("groups", "prefix"), "heads", None),
        P(("groups", "prefix"), None, "heads", None),
        P(("groups", "prefix"), None, "heads", None),
        P("groups"),
        P("groups"),
        P("groups"),
    )
    out_specs = P(("groups", "prefix"), "heads", "sub", None)
    return jax.shard_map(local, mesh=mesh, in_specs=in_specs, out_specs=out_specs, check_vma=False)
```

```python
import functools
import math

import jax
import jax.numpy as jnp
from jax import lax
from jax.experimental import pallas as pl
from jax.experimental.pallas import tpu as pltpu
from jax.sharding import PartitionSpec as P


MOST = 8
NEG = -1e30
LOG2E = 1.4426950408889634


def nt_dot(a, b):
    return lax.dot_general(a, b, (((1,), (1,)), ((), ())), preferred_element_type=jnp.float32)


def split_three(x):
    high = x.astype(jnp.bfloat16)
    rest = x - high.astype(jnp.float32)
    middle = rest.astype(jnp.bfloat16)
    low = (rest - middle.astype(jnp.float32)).astype(jnp.bfloat16)
    return high, middle, low


def prefix_pass(q_ref, k_ref, v_ref, acc, den, top, scale, arrive):
    rows, kh, gs, hd = q_ref.shape
    plen = k_ref.shape[1]
    part = min(plen, 1024)
    pieces = plen // part
    stages = [(h, c) for h in range(kh) for c in range(pieces)]

    def score(stage):
        h, c = stage
        if c == 0:
            arrive(h)
        q = q_ref[:, h].reshape(rows * gs, hd)
        return nt_dot(q, k_ref[h, pl.ds(c * part, part), :])

    ready = score(stages[0])
    held = []
    for index, (h, c) in enumerate(stages):
        s = ready
        if index + 1 < len(stages):
            ready = score(stages[index + 1])
        m = jnp.max(s, axis=1, keepdims=True) * scale
        p = jnp.exp2(s * scale - m).astype(jnp.bfloat16)
        v = v_ref[h, pl.ds(c * part, part), :]
        pv = jnp.dot(
            p, jnp.concatenate([v, jnp.ones_like(v)], axis=1),
            preferred_element_type=jnp.float32,
        )
        held.append((m, pv))
        if c == pieces - 1:
            m, pv = held[0]
            for m_more, pv_more in held[1:]:
                joined = jnp.maximum(m, m_more)
                pv = pv * jnp.exp2(m - joined) + pv_more * jnp.exp2(m_more - joined)
                m = joined
            held = []
            acc[:, h] = pv[:, :hd].reshape(rows, gs, hd)
            den[:, h] = pv[:, hd:].reshape(rows, gs, hd)
            top[:, h] = jnp.broadcast_to(m, (rows * gs, hd)).reshape(rows, gs, hd)


def own_prefix_kernel(q_ref, k_hbm, v_hbm, acc, den, top, k_all, v_all, sems, *, scale):
    kh = q_ref.shape[1]

    def copies(h):
        return (
            pltpu.make_async_copy(k_hbm.at[h], k_all.at[h], sems.at[0, h]),
            pltpu.make_async_copy(v_hbm.at[h], v_all.at[h], sems.at[1, h]),
        )

    for h in range(kh):
        for copy in copies(h):
            copy.start()

    def arrive(h):
        for copy in copies(h):
            copy.wait()

    prefix_pass(q_ref, k_all, v_all, acc, den, top, scale, arrive)


def own_prefix(q, kh_arr, vh_arr):
    rows, heads, gs, hd = q.shape
    plen = kh_arr.shape[1]
    vmem = pl.BlockSpec(memory_space=pltpu.VMEM)
    hbm = pl.BlockSpec(memory_space=pltpu.HBM)
    return pl.pallas_call(
        functools.partial(own_prefix_kernel, scale=LOG2E / math.sqrt(hd)),
        in_specs=[vmem, hbm, hbm],
        out_specs=[vmem] * 5,
        scratch_shapes=[pltpu.SemaphoreType.DMA((2, heads))],
        out_shape=[jax.ShapeDtypeStruct(q.shape, jnp.float32)] * 3
        + [jax.ShapeDtypeStruct(kh_arr.shape, jnp.bfloat16)] * 2,
        cost_estimate=pl.CostEstimate(
            flops=8 * rows * heads * gs * hd * plen,
            bytes_accessed=4 * plen * heads * hd,
            transcendentals=rows * heads * gs * plen,
        ),
        compiler_params=pltpu.CompilerParams(vmem_limit_bytes=46 * 1024 * 1024),
    )(q, kh_arr, vh_arr)


def block_kernel(
    meta, q_ref, k_ref, v_ref, sk_hbm, sv_hbm, *rest, slots, chunk, scale, home_block
):
    if home_block:
        acc_in, den_in, top_in = k_ref, v_ref, rest[0]
        o_ref, lse_ref, acc, top, den, kbuf, vbuf, tasks, sems = rest[1:]
    else:
        o_ref, acc, top, den, kbuf, vbuf, tasks, sems = rest
    rows, kh, gs, hd = q_ref.shape
    first = meta[3 * slots]
    wide = chunk * kh
    window = MOST * gs
    depth = kbuf.shape[0]

    def copies(task, buf):
        slot = tasks[task, 0]
        base = tasks[task, 1] * wide
        src = pl.ds(pl.multiple_of(base, wide), wide)
        return (
            pltpu.make_async_copy(sk_hbm.at[slot, src], kbuf.at[buf], sems.at[0, buf]),
            pltpu.make_async_copy(sv_hbm.at[slot, src], vbuf.at[buf], sems.at[1, buf]),
        )

    total = jnp.int32(0)
    for slot in range(slots):
        begin = meta[slot]
        amount = meta[slots + slot]
        past = meta[2 * slots + slot]
        touches = (begin < first + rows) & (begin + amount > first)
        reach = jnp.where(touches, past + amount, 0)
        blocks = (reach + chunk - 1) // chunk

        def put(i, count, slot=slot):
            tasks[count, 0] = slot
            tasks[count, 1] = i
            return count + 1

        total = lax.fori_loop(0, blocks, put, total)

    for ahead in range(depth - 1):

        @pl.when(ahead < total)
        def _(ahead=ahead):
            for copy in copies(ahead, ahead):
                copy.start()

    if home_block:
        acc[...] = acc_in[...]
        den[...] = den_in[...]
        top[...] = top_in[...]
    else:
        prefix_pass(q_ref, k_ref, v_ref, acc, den, top, scale, lambda h: None)

    unit = 256 if wide % 256 == 0 else wide
    per = unit // kh
    i_at = lax.broadcasted_iota(jnp.int32, (unit, unit), 0)
    j_at = lax.broadcasted_iota(jnp.int32, (unit, unit), 1)
    sort = jnp.where(lax.rem(i_at, per) * kh + i_at // per == j_at, 1.0, 0.0)
    sort = sort.astype(jnp.bfloat16)
    i_row = lax.broadcasted_iota(jnp.int32, (window, 1), 0) // gs
    pos = lax.broadcasted_iota(jnp.int32, (1, chunk), 1)

    def by_head(ref, buf):
        groups = [
            jnp.dot(
                sort, ref[buf, pl.ds(g * unit, unit), :], preferred_element_type=jnp.float32
            ).astype(jnp.bfloat16)
            for g in range(wide // unit)
        ]
        return [
            jnp.concatenate([group[h * per : (h + 1) * per] for group in groups], axis=0)
            for h in range(kh)
        ]

    def body(t, carry):
        buf = lax.rem(t, depth)

        @pl.when(t + depth - 1 < total)
        def _():
            for copy in copies(t + depth - 1, lax.rem(t + depth - 1, depth)):
                copy.start()

        slot = tasks[t, 0]
        base = tasks[t, 1] * chunk
        begin = meta[slot]
        amount = meta[slots + slot]
        past = meta[2 * slots + slot]
        start = jnp.clip(begin - first, 0, rows - MOST)
        place = i_row + (first + start - begin)
        limit = jnp.where((place >= 0) & (place < amount), past + place + 1, 0) - base
        allowed = pos < limit
        rows_at = pl.ds(start, MOST)
        for copy in copies(t, buf):
            copy.wait()
        keys = by_head(kbuf, buf)
        scores = [
            nt_dot(q_ref[rows_at, h].reshape(window, hd), keys[h]) for h in range(kh)
        ]
        values = by_head(vbuf, buf)
        shape = (MOST, gs, hd)
        for h in range(kh):
            s = jnp.where(allowed, scores[h], NEG)
            old_top = top[rows_at, h].reshape(window, hd)
            m = jnp.maximum(old_top, jnp.max(s, axis=1, keepdims=True) * scale)
            p = jnp.exp2(s * scale - m[:, :1]).astype(jnp.bfloat16)
            v = values[h]
            pv = jnp.dot(
                p, jnp.concatenate([v, jnp.ones_like(v)], axis=1),
                preferred_element_type=jnp.float32,
            )
            factor = jnp.exp2(old_top - m)
            top[rows_at, h] = m.reshape(shape)
            den[rows_at, h] = (
                den[rows_at, h].reshape(window, hd) * factor + pv[:, hd:]
            ).reshape(shape)
            acc[rows_at, h] = (
                acc[rows_at, h].reshape(window, hd) * factor + pv[:, :hd]
            ).reshape(shape)
        return carry

    lax.fori_loop(0, total, body, 0)
    d = den[...]
    out = (acc[...] / d).astype(o_ref.dtype)
    lse = (top[...] + jnp.log2(d)).reshape(rows * kh * gs // hd, hd, hd)
    eye = lax.broadcasted_iota(jnp.int32, (1, hd, hd), 1) == lax.broadcasted_iota(
        jnp.int32, (1, hd, hd), 2
    )
    lse = jnp.sum(jnp.where(eye, lse, 0.0), axis=1)
    if home_block:
        o_ref[...] = out
        lse_ref[...] = lse
    else:
        tiles = -(-lse.shape[0] // gs)
        padding = tiles * gs - lse.shape[0]
        if padding:
            lse = jnp.concatenate([lse, jnp.zeros((padding, hd), lse.dtype)], axis=0)
        o_ref[pl.ds(0, rows)] = out
        pieces = []
        for piece in split_three(lse):
            piece = piece.reshape(tiles, gs, hd)
            pieces.append(piece)
        flat = jnp.concatenate(pieces, axis=0)
        spare = (o_ref.shape[0] - rows) * kh - flat.shape[0]
        if spare:
            flat = jnp.concatenate([flat, jnp.zeros((spare, gs, hd), flat.dtype)], axis=0)
        o_ref[pl.ds(rows, o_ref.shape[0] - rows)] = flat.reshape(
            o_ref.shape[0] - rows, kh, gs, hd
        )


def stat_rows(shape):
    rows, heads, gs, hd = shape
    tiles = 3 * -(-(rows * heads * gs // hd) // gs)
    return -(-tiles // heads)


def block_part(q, home, table, first_in, second_in, sk, sv, third_in=None):
    rows, heads, gs, hd = q.shape
    home_block = third_in is not None
    plen = 0 if home_block else first_in.shape[1]
    slots, flat, _ = sk.shape
    slen = flat // heads
    chunk = min(slen, 256)
    meta = jnp.concatenate([table, (home * rows)[None].astype(jnp.int32)])
    most_tasks = slots * (slen // chunk)
    state = pltpu.VMEM((rows, heads, gs, hd), jnp.float32)
    kernel = functools.partial(
        block_kernel,
        slots=slots,
        chunk=chunk,
        scale=LOG2E / math.sqrt(hd),
        home_block=home_block,
    )
    if home_block:
        out_shape = [
            jax.ShapeDtypeStruct(q.shape, jnp.float32),
            jax.ShapeDtypeStruct((rows * heads * gs // hd, hd), jnp.float32),
        ]
    else:
        out_shape = [
            jax.ShapeDtypeStruct((rows + stat_rows(q.shape), heads, gs, hd), jnp.bfloat16)
        ]
    vmem = pl.BlockSpec(memory_space=pltpu.VMEM)
    hbm = pl.BlockSpec(memory_space=pltpu.HBM)
    more = [vmem] if home_block else []
    last = [third_in] if home_block else []
    return pl.pallas_call(
        kernel,
        in_specs=[pl.BlockSpec(memory_space=pltpu.SMEM), vmem, vmem, vmem, hbm, hbm] + more,
        out_specs=[vmem] * len(out_shape),
        scratch_shapes=[
            state,
            state,
            state,
            pltpu.VMEM((4, chunk * heads, hd), jnp.bfloat16),
            pltpu.VMEM((4, chunk * heads, hd), jnp.bfloat16),
            pltpu.SMEM((most_tasks, 2), jnp.int32),
            pltpu.SemaphoreType.DMA((2, 4)),
        ],
        out_shape=out_shape,
        cost_estimate=pl.CostEstimate(
            flops=8 * rows * heads * gs * hd * plen,
            bytes_accessed=4 * plen * heads * hd + 4 * slots * flat * hd // 4,
            transcendentals=rows * heads * gs * plen,
        ),
        compiler_params=pltpu.CompilerParams(vmem_limit_bytes=46 * 1024 * 1024),
    )(meta, q, first_in, second_in, sk, sv, *last)


def merge_kernel(*refs):
    own, own_lse = refs[0], refs[1]
    others = refs[2:-1]
    result = refs[-1]
    rows, heads, gs, hd = result.shape
    total_rows = rows * heads * gs
    groups = total_rows // hd
    tiles = -(-groups // gs)
    lses = [own_lse[...]]
    for ref in others:
        flat = ref[pl.ds(rows, ref.shape[0] - rows)].astype(jnp.float32)
        flat = flat.reshape((ref.shape[0] - rows) * heads, gs, hd)
        high, middle, low = (flat[i * tiles : (i + 1) * tiles] for i in range(3))
        lses.append((high + middle + low).reshape(tiles * gs, hd)[:groups])
    highest = lses[0]
    for lse in lses[1:]:
        highest = jnp.maximum(highest, lse)
    weights = [jnp.exp2(lse - highest) for lse in lses]
    total = sum(weights)
    eye = lax.broadcasted_iota(jnp.int32, (1, hd, hd), 1) == lax.broadcasted_iota(
        jnp.int32, (1, hd, hd), 2
    )
    summed = jnp.zeros((total_rows, hd), jnp.float32)
    for ref, weight in zip((own,) + tuple(others), weights):
        lanes = jnp.broadcast_to((weight / total)[:, None, :], (groups, hd, hd))
        column = jnp.sum(jnp.where(eye, lanes, 0.0), axis=2, keepdims=True)
        column = column.reshape(total_rows, 1)
        block = ref[pl.ds(0, rows)].astype(jnp.float32).reshape(total_rows, hd)
        summed = summed + block * column
    result[...] = summed.astype(result.dtype).reshape(result.shape)


def merged(own, own_lse, others, shape):
    return pl.pallas_call(
        merge_kernel,
        out_shape=jax.ShapeDtypeStruct(shape, jnp.bfloat16),
        compiler_params=pltpu.CompilerParams(vmem_limit_bytes=46 * 1024 * 1024),
    )(own, own_lse, *others)


def owned_requests(accepted, cache_slot, history, owner_index, held_slots):
    request_ends = jnp.cumsum(accepted)
    starts = request_ends - accepted
    wanted = owner_index * held_slots + jnp.arange(held_slots, dtype=jnp.int32)
    matches = (cache_slot[None, :] == wanted[:, None]).astype(jnp.int32)
    data = jnp.stack([starts, accepted, history])
    return jnp.sum(matches[None] * data[:, None, :], axis=2).reshape(-1)


def shifted(value, steps):
    count = lax.axis_size("prefix")
    pairs = [(source, (source + steps) % count) for source in range(count)]
    return lax.ppermute(value, "prefix", pairs)


def local(
    queries, prefix_keys, prefix_values, suffix_keys, suffix_values, accepted, cache_slot, history
):
    owner = lax.axis_index("prefix")
    parties = lax.axis_size("prefix")
    slots, slen, heads, hd = suffix_keys.shape
    arrived = [queries] + [shifted(queries, step) for step in range(1, parties)]
    table = owned_requests(accepted, cache_slot, history, owner, slots)
    kh = prefix_keys.transpose(1, 0, 2)
    vh = prefix_values.transpose(1, 0, 2)
    sk = suffix_keys.reshape(slots, slen * heads, hd)
    sv = suffix_values.reshape(slots, slen * heads, hd)
    acc, den, top, kh, vh = own_prefix(queries, kh, vh)
    acc, den, top, table = lax.optimization_barrier((acc, den, top, table))
    others = []
    for step in range(1, parties):
        home = (owner - step) % parties
        (out,) = block_part(arrived[step], home, table, kh, vh, sk, sv)
        others.append(shifted(out, -step))
    own, own_lse = block_part(queries, owner, table, acc, den, sk, sv, top)
    return merged(own, own_lse, others, queries.shape)


def solution(mesh):
    in_specs = (
        P(("groups", "prefix"), "heads", "sub", None),
        P(("groups", "prefix"), "heads", None),
        P(("groups", "prefix"), "heads", None),
        P(("groups", "prefix"), None, "heads", None),
        P(("groups", "prefix"), None, "heads", None),
        P("groups"),
        P("groups"),
        P("groups"),
    )
    out_specs = P(("groups", "prefix"), "heads", "sub", None)
    return jax.shard_map(local, mesh=mesh, in_specs=in_specs, out_specs=out_specs, check_vma=False)
```
